32 devices in a mesh: grp: 2 (over x), wide: 16 (over z, y, core).
Axes of the slice: x: 2, y: 2, z: 4, core: 2. Of those that a mesh axis runs over, the one named last changes fastest.
Arguments:
- queries: bfloat16 [256, 4096], P(('grp', 'wide')), parts along dimension 0, may hold values from -8 to 8
- draft_keys: bfloat16 [256, 512], P(('grp', 'wide')), parts along dimension 0, may hold values from -8 to 8
- draft_values: bfloat16 [256, 512], P(('grp', 'wide')), parts along dimension 0, may hold values from -24 to 24
- cache_keys: bfloat16 [262144, 128], P(('grp', 'wide')), parts along dimension 0, may hold values from -8 to 8
- cache_values: bfloat16 [262144, 128], P(('grp', 'wide')), parts along dimension 0, may hold values from -24 to 24
- block_owner: int32 [32], P('grp'), parts along dimension 0, may hold values from 0 to 15, each once
- block_lengths: int32 [32], P('grp'), parts along dimension 0, may hold values from 1024 to 8192, as said below
- draft_mask: int32 [4, 64, 64], P('grp'), parts along dimension 0, may hold values from 0 to 1, as said below
- out_weight: bfloat16 [4096, 8192], P(None, 'wide'), may hold values from -1 to 1
- norm_gain: float32 [8192], replicated, may hold values from 0.25 to 1.75
- gate_weight: bfloat16 [8192, 14336], P(None, 'wide'), may hold values from -0.0625 to 0.0625
- up_weight: bfloat16 [8192, 14336], P(None, 'wide'), may hold values from -0.0625 to 0.0625
Outputs:
- projected: bfloat16 [256, 8192], P('grp', 'wide'), parts along dimension 0
- hidden: bfloat16 [256, 14336], P('grp', 'wide'), parts along dimension 0
The draws below stay inside these ranges and needn't reach their ends.
There are 2 independent parts, one for each index of `grp`. The reference program is written for one: setup_inputs(seed, part) draws one part's arguments, and reference() takes and returns one part's arrays. A program takes and returns all parts, laid end to end along the dimension named above; an argument that names none is the same for every part. Nothing has to cross between parts.
Inputs may be any that keep to these rules, and one draw needn't show every extreme that they name: `block_owner`: each device holds exactly one block. `block_lengths`: at most 8192 rows a block, and some block has exactly 8192 rows. In each sequence row 0 is the root of a tree in which every other row's parent lies 1 to 4 rows before it; draft_mask[s, i, t] is 1 exactly when t is i or an ancestor of i.
All inputs are finite; a program needn't handle non-finite values.
Results may differ from the reference program's by a relative error of at most 0.02.
Values may be sent and summed in bfloat16 or wider, within the bound.
No kernel may reach another device: no remote copies, remote signals or barrier semaphores. Data moves between devices by JAX's collectives and lax.ppermute only.
A program may use at most 128 MiB of HBM per device.

```python
import math
import jax
import jax.numpy as jnp
from jax import lax

D = 8192
KVH = 4
GROUP = 8
HD = 128
FF = 14336
SEQS = 2
DRAFT = 64
CAP = 8192
ROWS = 128
N_WIDE = 16


def draw_queries(key, part):
    own = jax.random.fold_in(key, 101)
    shape = (ROWS, KVH * GROUP * HD)
    base = jnp.clip(2.0 * jax.random.normal(own, shape, jnp.float32), -8.0, 8.0)
    return base.astype(jnp.bfloat16)


def draw_cache_keys(key, part):
    own = jax.random.fold_in(key, 202)
    shape = (N_WIDE * CAP, HD)
    base = jnp.clip(jax.random.normal(own, shape, jnp.float32), -8.0, 8.0)
    return base.astype(jnp.bfloat16)


def draw_block_lengths(key, part):
    first, second, third = jax.random.split(jax.random.fold_in(key, 303), 3)
    left = jax.random.randint(first, (N_WIDE,), 0, CAP, jnp.int32)
    right = jax.random.randint(second, (N_WIDE,), 0, CAP, jnp.int32)
    lengths = CAP // 8 + left * right // CAP * 7 // 8
    chosen = jax.random.randint(third, (), 0, N_WIDE, jnp.int32)
    return jnp.where(jnp.arange(N_WIDE, dtype=jnp.int32) == chosen, CAP, lengths).astype(jnp.int32)


def draw_draft_mask(key, part):
    steps_back = jax.random.randint(jax.random.fold_in(key, 404), (SEQS, DRAFT), 1, 5, jnp.int32)
    index = jnp.arange(DRAFT, dtype=jnp.int32)
    parent = jnp.maximum(index[None, :] - steps_back, 0)
    link = (index[None, None, :] == parent[:, :, None]) & (index[None, :, None] > 0)
    reach = link.astype(jnp.int32) + jnp.eye(DRAFT, dtype=jnp.int32)[None]
    levels = int(math.log2(DRAFT)) + 1
    for repeat in range(levels):
        reach = jnp.minimum(jnp.matmul(reach, reach), 1)
    return reach.astype(jnp.int32)


def draw_out_weight(key, part):
    first, second = jax.random.split(jax.random.fold_in(key, 505))
    fan_width = KVH * GROUP * HD
    entries = jax.random.normal(first, (fan_width, D), jnp.float32) / math.sqrt(fan_width)
    spread = jnp.exp(jax.random.uniform(second, (D,), jnp.float32, 0.0, math.log(10.0)))
    position = jnp.arange(D, dtype=jnp.float32) / D
    ramp = jnp.exp(position * math.log(3.0))
    return jnp.clip(entries * (spread * ramp / 8.0)[None, :], -1.0, 1.0).astype(jnp.bfloat16)


def block_scale(key, dims, cuts, smallest, largest):
    def one(dim, parts):
        draws = jax.random.uniform(jax.random.fold_in(jax.random.fold_in(key, 6), dim), (parts,), jnp.float32, smallest / len(cuts), largest / len(cuts))
        return jnp.repeat(jnp.exp(draws), dims[dim] // parts).reshape((-1,) + (1,) * (len(dims) - dim - 1))

    loudness = one(*cuts[0])
    for cut in cuts[1:]:
        loudness = loudness * one(*cut)
    return loudness


def noise(rng, extent, deviation, most, cuts=(), held_as=jnp.bfloat16):
    gain = block_scale(rng, extent, cuts, -0.22, 0.18) if cuts else 1.0
    result = jax.random.normal(rng, extent, jnp.float32) * deviation * gain
    return jnp.minimum(jnp.maximum(result, -most), most).astype(held_as)


def setup_inputs(seed: int = 0, part: int = 0) -> dict:
    key_of = jax.random.split(jax.random.key(seed), 13)
    part_splits = jax.random.split(jax.random.fold_in(key_of[12], part), 13)
    return {
        "queries": draw_queries(jax.random.fold_in(jax.random.fold_in(key_of[12], part), 71), part),
        "draft_keys": noise(part_splits[1], (ROWS, KVH * HD), 2.0, 8.0, ((0, 16),)),
        "draft_values": noise(part_splits[2], (ROWS, KVH * HD), 4.0, 24.0, ((0, 16),)),
        "cache_keys": draw_cache_keys(jax.random.fold_in(jax.random.fold_in(key_of[12], part), 71), part),
        "cache_values": noise(part_splits[4], (N_WIDE * CAP, HD), 4.0, 24.0, ((0, 16),)),
        "block_owner": jax.random.permutation(part_splits[5], N_WIDE).astype(jnp.int32),
        "block_lengths": draw_block_lengths(jax.random.fold_in(jax.random.fold_in(key_of[12], part), 71), part),
        "draft_mask": draw_draft_mask(jax.random.fold_in(jax.random.fold_in(key_of[12], part), 71), part),
        "out_weight": draw_out_weight(jax.random.fold_in(key_of[12], 71), part),
        "norm_gain": jnp.clip(1.0 + 0.15 * jax.random.normal(key_of[9], (D,), jnp.float32), 0.25, 1.75),
        "gate_weight": noise(key_of[10], (D, FF), D ** -0.5, 0.0625, ((1, 16),)),
        "up_weight": noise(key_of[11], (D, FF), D ** -0.5, 0.0625, ((1, 16),)),
    }


very_low = -1e+30
epsilon = 1e-05

def block_update(state, query_rows, block_keys, block_values, valid, scale):
    running, total, weighted = state
    scores = jnp.einsum('igc,kc->igk', query_rows.astype(jnp.float32), block_keys.astype(jnp.float32), precision=lax.Precision.HIGHEST) * scale
    scores = jnp.where(valid, scores, very_low)
    newest = jnp.maximum(running, lax.optimization_barrier(jnp.max(scores, axis=-1)))
    factor = jnp.exp(running - newest)
    weights = jnp.where(valid, jnp.exp(scores - newest[..., None]), 0.0)
    total = total * factor + lax.optimization_barrier(jnp.sum(weights, axis=-1))
    rounded = lax.optimization_barrier(weights.astype(jnp.bfloat16))
    weighted = weighted * factor[..., None] + jnp.einsum('igk,kc->igc', rounded.astype(jnp.float32), block_values.astype(jnp.float32), precision=lax.Precision.HIGHEST)
    return (newest, total, weighted)

def attend(query_rows, keys, values, length, own_keys, own_values, own_valid):
    block_size = min(512, keys.shape[0])
    scale = 1.0 / math.sqrt(query_rows.shape[2])
    rows_count = query_rows.shape[0]
    heads = query_rows.shape[1]
    state = (jnp.full((rows_count, heads), very_low, jnp.float32), jnp.zeros((rows_count, heads), jnp.float32), jnp.zeros((rows_count, heads, query_rows.shape[2]), jnp.float32))
    offsets = jnp.arange(block_size, dtype=jnp.int32)

    def advance(number, carry):
        begin = (number * block_size).astype(jnp.int32)
        block_keys = lax.dynamic_slice_in_dim(keys, begin, block_size, 0)
        block_values = lax.dynamic_slice_in_dim(values, begin, block_size, 0)
        valid = (begin + offsets < length)[None, None, :]
        return block_update(carry, query_rows, block_keys, block_values, valid, scale)
    count = ((length + block_size - 1) // block_size).astype(jnp.int32)
    state = lax.fori_loop(jnp.int32(0), count, advance, state)
    return block_update(state, query_rows, own_keys, own_values, own_valid[:, None, :], scale)

def reference(queries, draft_keys, draft_values, cache_keys, cache_values, block_owner, block_lengths, draft_mask, out_weight, norm_gain, gate_weight, up_weight):
    blocks_per_pair = N_WIDE // (SEQS * KVH)
    group_width = GROUP * HD

    def one_pair(pair):
        sequence = pair // KVH
        head = pair % KVH
        row_start = (sequence * DRAFT).astype(jnp.int32)
        rows = lax.dynamic_slice_in_dim(lax.dynamic_slice_in_dim(queries, row_start, DRAFT, 0), (head * group_width).astype(jnp.int32), group_width, 1).reshape(DRAFT, GROUP, HD)
        own_keys = lax.dynamic_slice_in_dim(lax.dynamic_slice_in_dim(draft_keys, row_start, DRAFT, 0), (head * HD).astype(jnp.int32), HD, 1)
        own_values = lax.dynamic_slice_in_dim(lax.dynamic_slice_in_dim(draft_values, row_start, DRAFT, 0), (head * HD).astype(jnp.int32), HD, 1)
        visible = lax.dynamic_index_in_dim(draft_mask, sequence, 0, keepdims=False) > 0

        def one_block(position):
            index = (pair * blocks_per_pair + position).astype(jnp.int32)
            owner = lax.dynamic_index_in_dim(block_owner, index, 0, keepdims=False)
            length = lax.dynamic_index_in_dim(block_lengths, index, 0, keepdims=False)
            keys = lax.dynamic_slice_in_dim(cache_keys, (owner * CAP).astype(jnp.int32), CAP, 0)
            values = lax.dynamic_slice_in_dim(cache_values, (owner * CAP).astype(jnp.int32), CAP, 0)
            valid = visible & (position == blocks_per_pair - 1)
            peak, total, weighted = attend(rows, keys, values, length, own_keys, own_values, valid)
            output = lax.optimization_barrier((weighted / total[..., None]).astype(jnp.bfloat16)).astype(jnp.float32)
            return (peak, total, output)
        maxima, totals, outputs = lax.map(one_block, jnp.arange(blocks_per_pair, dtype=jnp.int32))
        highest = lax.optimization_barrier(jnp.max(maxima, axis=0))
        mixing = jnp.exp(maxima - highest[None]) * totals
        total = lax.optimization_barrier(jnp.sum(mixing, axis=0))
        weighted = lax.optimization_barrier(jnp.sum(mixing[..., None] * outputs, axis=0))
        return (weighted / total[..., None]).astype(jnp.bfloat16)
    pairs = lax.map(one_pair, jnp.arange(SEQS * KVH, dtype=jnp.int32))
    attended = pairs.reshape(SEQS, KVH, DRAFT, GROUP * HD).transpose(0, 2, 1, 3).reshape(SEQS * DRAFT, KVH * GROUP * HD)
    projected = jnp.dot(attended, out_weight, preferred_element_type=jnp.float32).astype(jnp.bfloat16)
    branch = lax.optimization_barrier(projected).astype(jnp.float32)
    inverse = lax.rsqrt(lax.optimization_barrier(jnp.sum(branch * branch, axis=1)) / D + epsilon)
    normed = (branch * inverse[:, None] * norm_gain[None, :]).astype(jnp.bfloat16)
    gate = jnp.dot(normed, gate_weight, preferred_element_type=jnp.float32)
    upward = jnp.dot(normed, up_weight, preferred_element_type=jnp.float32)
    hidden = (jax.nn.silu(gate) * upward).astype(jnp.bfloat16)
    return (projected, hidden)
```

```python
import functools
import math

import jax
import jax.numpy as jnp
from jax import lax
from jax.experimental import pallas as pl
from jax.experimental.pallas import tpu as pltpu
from jax.sharding import PartitionSpec as P

very_low = -1e30
epsilon = 1e-05
log2e = 1.4426950408889634
lanes = 128


def attention_kernel(
    sequences, rows, group, head_size, info, recv, mask, keys, values, out, land, q, top, total, acc, sem
):
    step = pl.program_id(0)
    block = keys.shape[0]
    length, own_sequence, is_last = info[0], info[1], info[2]
    scale = log2e / math.sqrt(head_size)
    width = group * head_size

    def fold(scores, valid, block_values):
        if valid is not None:
            scores = jnp.where(valid, scores, very_low)
        peak = top[...]
        newest = jnp.maximum(peak, jnp.max(scores, axis=1, keepdims=True))
        factor = jnp.exp2(peak - newest)
        part, weights = None, []
        for at in range(0, scores.shape[1], lanes):
            tile = jnp.exp2(scores[:, at : at + lanes] - newest)
            if valid is not None:
                tile = jnp.where(valid[:, at : at + lanes], tile, 0.0)
            part = tile if part is None else part + tile
            weights.append(tile.astype(jnp.bfloat16))
        total[...] = total[...] * factor + part
        acc[...] = acc[...] * factor + jnp.dot(
            jnp.concatenate(weights, axis=1), block_values, preferred_element_type=jnp.float32
        )
        top[...] = newest

    def score(block_keys):
        return (
            lax.dot_general(
                q[...], block_keys, (((1,), (1,)), ((), ())), preferred_element_type=jnp.float32
            )
            * scale
        )

    @pl.when(step == 0)
    def _():
        sources = recv.shape[0] // sequences
        copy = pltpu.make_async_copy(recv.at[pl.ds(own_sequence * sources, sources)], land, sem)
        copy.start()
        copy.wait()
        mine = land[...].reshape(rows, land.shape[2])
        for head in range(group):
            q[head * rows : (head + 1) * rows, :] = mine[:, head * head_size : (head + 1) * head_size]
        own_keys = jnp.concatenate(
            [mine[:, width : width + head_size], jnp.zeros((lanes - rows, head_size), jnp.bfloat16)], 0
        )
        own_values = jnp.concatenate(
            [
                mine[:, width + head_size : width + 2 * head_size],
                jnp.zeros((lanes - rows, head_size), jnp.bfloat16),
            ],
            0,
        )
        seen = jnp.where(is_last > 0, mask[0].astype(jnp.float32), 0.0)
        seen = jnp.concatenate([seen, jnp.zeros((rows, lanes - rows), jnp.float32)], 1)
        valid = jnp.concatenate([seen] * group, 0) > 0.0
        top[...] = jnp.full_like(top, very_low)
        total[...] = jnp.zeros_like(total)
        acc[...] = jnp.zeros_like(acc)
        fold(score(own_keys), valid, own_values)

    @pl.when((step + 1) * block <= length)
    def _():
        fold(score(keys[...]), None, values[...])

    @pl.when((step * block < length) & ((step + 1) * block > length))
    def _():
        at = step * block + lax.broadcasted_iota(jnp.int32, (1, block), 1)
        valid = jnp.broadcast_to(at < length, (q.shape[0], block))
        fold(score(keys[...]), valid, values[...])

    @pl.when(step == pl.num_programs(0) - 1)
    def _():
        summed = jnp.sum(total[...], axis=1, keepdims=True)
        result = acc[...] / summed
        level = top[...] + jnp.log2(summed)
        lane = lax.broadcasted_iota(jnp.int32, (rows, lanes), 1)
        notes = jnp.zeros((rows, lanes), jnp.float32)
        for head in range(group):
            part = slice(head * rows, (head + 1) * rows)
            out[:, head * head_size : (head + 1) * head_size] = result[part].astype(jnp.bfloat16)
            rest = jnp.broadcast_to(level[part, :1], (rows, lanes))
            for piece in range(3):
                cut = rest.astype(jnp.bfloat16).astype(jnp.float32)
                notes = jnp.where(lane == piece * group + head, cut, notes)
                rest = rest - cut
        out[:, width:] = notes.astype(jnp.bfloat16)


def attention(info, recv, mask, keys, values, group):
    head_size = keys.shape[1]
    sequences, rows = mask.shape[0], mask.shape[1]
    capacity = keys.shape[0]
    block = min(1024, capacity)
    width = group * head_size

    def at(step, info):
        return (jnp.minimum(step, (info[0] + block - 1) // block - 1), 0)

    return pl.pallas_call(
        functools.partial(attention_kernel, sequences, rows, group, head_size),
        out_shape=jax.ShapeDtypeStruct((rows, width + lanes), jnp.bfloat16),
        grid_spec=pltpu.PrefetchScalarGridSpec(
            num_scalar_prefetch=1,
            grid=(capacity // block,),
            in_specs=[
                pl.BlockSpec(memory_space=pl.ANY),
                pl.BlockSpec((1, rows, rows), lambda step, info: (info[1], 0, 0)),
                pl.BlockSpec((block, head_size), at),
                pl.BlockSpec((block, head_size), at),
            ],
            out_specs=pl.BlockSpec((rows, width + lanes), lambda step, info: (0, 0)),
            scratch_shapes=[
                pltpu.VMEM((recv.shape[0] // sequences,) + recv.shape[1:], recv.dtype),
                pltpu.VMEM((group * rows, head_size), jnp.bfloat16),
                pltpu.VMEM((group * rows, lanes), jnp.float32),
                pltpu.VMEM((group * rows, lanes), jnp.float32),
                pltpu.VMEM((group * rows, head_size), jnp.float32),
                pltpu.SemaphoreType.DMA,
            ],
        ),
        compiler_params=pltpu.CompilerParams(vmem_limit_bytes=48 << 20),
        cost_estimate=pl.CostEstimate(
            flops=4 * group * rows * capacity * head_size,
            bytes_accessed=4 * capacity * head_size,
            transcendentals=group * rows * capacity,
        ),
        name="attention",
    )(info, recv, mask, keys, values)


def projection_kernel(pieces, per_pair, key_heads, sequences, group, head_size, *refs):
    where_from = refs[0]
    blocks = refs[1 : 1 + pieces]
    weight = refs[1 + pieces]
    out = refs[2 + pieces]
    held, weight_held, attended, piece_sem, weight_sem = refs[3 + pieces :]
    rows = held.shape[1]
    width = group * head_size
    copies = []
    for piece in range(pieces):
        copy = pltpu.make_async_copy(blocks[piece], held.at[piece], piece_sem.at[piece])
        copy.start()
        copies.append(copy)
    chunks = weight_sem.shape[0]
    depth = weight.shape[0] // chunks
    loads = []
    for chunk in range(chunks):
        part = pl.ds(chunk * depth, depth)
        copy = pltpu.make_async_copy(weight.at[part], weight_held.at[part], weight_sem.at[chunk])
        copy.start()
        loads.append(copy)
    for copy in copies:
        copy.wait()
    for head in range(key_heads):
        for sequence in range(sequences):
            pair = sequence * key_heads + head
            slots = [where_from[pair * per_pair + number] for number in range(per_pair)]
            levels = []
            for slot in slots:
                notes = held[slot, :, width:].astype(jnp.float32)
                levels.append(
                    notes
                    + pltpu.roll(notes, lanes - group, 1)
                    + pltpu.roll(notes, lanes - 2 * group, 1)
                )
            highest = functools.reduce(jnp.maximum, levels)
            mixing = [jnp.exp2(level - highest) for level in levels]
            whole = functools.reduce(jnp.add, mixing)
            mixing = [part / whole for part in mixing]
            for member in range(group):
                columns = slice(member * head_size, (member + 1) * head_size)
                gathered = None
                for slot, part in zip(slots, mixing):
                    term = part[:, member : member + 1] * held[slot, :, columns].astype(jnp.float32)
                    gathered = term if gathered is None else gathered + term
                attended[
                    sequence * rows : (sequence + 1) * rows,
                    head * width + member * head_size : head * width + (member + 1) * head_size,
                ] = gathered.astype(jnp.bfloat16)
    result = None
    for chunk in range(chunks):
        loads[chunk].wait()
        part = slice(chunk * depth, (chunk + 1) * depth)
        term = jnp.dot(attended[:, part], weight_held[part, :], preferred_element_type=jnp.float32)
        result = term if result is None else result + term
    out[...] = result.astype(jnp.bfloat16)


def projection(where_from, blocks, weight, per_pair, key_heads, sequences, group, head_size):
    pieces = len(blocks)
    rows, extent = blocks[0].shape
    chunks = 4
    return pl.pallas_call(
        functools.partial(
            projection_kernel, pieces, per_pair, key_heads, sequences, group, head_size
        ),
        out_shape=jax.ShapeDtypeStruct((sequences * rows, weight.shape[1]), jnp.bfloat16),
        in_specs=[pl.BlockSpec(memory_space=pltpu.SMEM)]
        + [pl.BlockSpec(memory_space=pl.ANY)] * (pieces + 1),
        out_specs=pl.BlockSpec(memory_space=pltpu.VMEM),
        scratch_shapes=[
            pltpu.VMEM((pieces, rows, extent), jnp.bfloat16),
            pltpu.VMEM(weight.shape, jnp.bfloat16),
            pltpu.VMEM((sequences * rows, weight.shape[0]), jnp.bfloat16),
            pltpu.SemaphoreType.DMA((pieces,)),
            pltpu.SemaphoreType.DMA((chunks,)),
        ],
        compiler_params=pltpu.CompilerParams(vmem_limit_bytes=48 << 20),
        cost_estimate=pl.CostEstimate(
            flops=2 * sequences * rows * weight.size,
            bytes_accessed=2 * (weight.size + pieces * rows * extent),
            transcendentals=0,
        ),
        name="projection",
    )(where_from, *blocks, weight)


def feed_kernel(pieces, total_width, *refs):
    order = refs[0]
    blocks = refs[1 : 1 + pieces]
    gain, gate_weight, up_weight, out = refs[1 + pieces : 5 + pieces]
    held, gate, up, squares, sem = refs[5 + pieces :]
    step = pl.program_id(0)

    def copy_of(piece):
        return pltpu.make_async_copy(blocks[piece], held.at[piece], sem.at[piece])

    @pl.when(step == 0)
    def _():
        for piece in range(pieces):
            copy_of(piece).start()
        gate[...] = jnp.zeros_like(gate)
        up[...] = jnp.zeros_like(up)
        squares[...] = jnp.zeros_like(squares)
        for piece in range(pieces):
            copy_of(piece).wait()

    branch = held[step].astype(jnp.float32)
    square = branch * branch
    part = squares[...]
    for at in range(0, square.shape[1], lanes):
        part = part + square[:, at : at + lanes]
    squares[...] = part
    scaled = (branch * gain[0]).astype(jnp.bfloat16)
    gate[...] += jnp.dot(scaled, gate_weight[...], preferred_element_type=jnp.float32)
    up[...] += jnp.dot(scaled, up_weight[...], preferred_element_type=jnp.float32)

    @pl.when(step == pl.num_programs(0) - 1)
    def _():
        inverse = lax.rsqrt(jnp.sum(squares[...], axis=1, keepdims=True) / total_width + epsilon)
        opened = gate[...] * inverse
        out[...] = (opened / (1.0 + jnp.exp(-opened)) * (up[...] * inverse)).astype(jnp.bfloat16)


def feed(order, blocks, gain, gate_weight, up_weight):
    pieces = len(blocks)
    rows, depth = blocks[0].shape
    width = gate_weight.shape[1]
    return pl.pallas_call(
        functools.partial(feed_kernel, pieces, pieces * depth),
        out_shape=jax.ShapeDtypeStruct((rows, width), jnp.bfloat16),
        grid_spec=pltpu.PrefetchScalarGridSpec(
            num_scalar_prefetch=1,
            grid=(pieces,),
            in_specs=[pl.BlockSpec(memory_space=pl.ANY)] * pieces
            + [
                pl.BlockSpec((1, 1, depth), lambda step, order: (order[step], 0, 0)),
                pl.BlockSpec((depth, width), lambda step, order: (order[step], 0)),
                pl.BlockSpec((depth, width), lambda step, order: (order[step], 0)),
            ],
            out_specs=pl.BlockSpec((rows, width), lambda step, order: (0, 0)),
            scratch_shapes=[
                pltpu.VMEM((pieces, rows, depth), jnp.bfloat16),
                pltpu.VMEM((rows, width), jnp.float32),
                pltpu.VMEM((rows, width), jnp.float32),
                pltpu.VMEM((rows, lanes), jnp.float32),
                pltpu.SemaphoreType.DMA((pieces,)),
            ],
        ),
        compiler_params=pltpu.CompilerParams(vmem_limit_bytes=48 << 20),
        cost_estimate=pl.CostEstimate(
            flops=4 * rows * pieces * depth * width,
            bytes_accessed=4 * pieces * depth * width,
            transcendentals=rows * width,
        ),
        name="feed",
    )(order, *blocks, gain.reshape(pieces, 1, depth), gate_weight, up_weight)


def spread(block, devices):
    far = devices // 4

    def turn(value, number):
        return lax.ppermute(
            value, "wide", [(i, (i + 4 * number) % devices) for i in range(devices)]
        )

    def swap(value, bit):
        return lax.ppermute(value, "wide", [(i, i ^ bit) for i in range(devices)])

    found = [block] + [turn(block, number) for number in range(1, far)]
    found = found + [swap(value, 2) for value in found]
    return found + [swap(value, 1) for value in found]


def origins(devices, own_index):
    far = devices // 4
    number = jnp.arange(devices, dtype=jnp.int32)
    back, swapped = number % far, number // far
    return (own_index - 4 * back + devices) % devices ^ (swapped % 2 * 2 + swapped // 2)


def per_device(
    queries,
    draft_keys,
    draft_values,
    cache_keys,
    cache_values,
    block_owner,
    block_lengths,
    draft_mask,
    out_weight,
    norm_gain,
    gate_weight,
    up_weight,
):
    devices = lax.axis_size("wide")
    own_index = lax.axis_index("wide").astype(jnp.int32)
    head_size = cache_keys.shape[1]
    key_heads = draft_keys.shape[1] // head_size
    group_width = queries.shape[1] // key_heads
    group = group_width // head_size
    sequences = draft_mask.shape[0]
    local_rows = queries.shape[0]
    per_pair = devices // (sequences * key_heads)
    device_ids = jnp.arange(devices, dtype=jnp.int32)
    owned = (block_owner[None, :] == device_ids[:, None]).astype(jnp.int32)
    device_block = jnp.sum(owned * device_ids[None, :], axis=1)
    device_head = device_block // per_pair % key_heads
    mine = (block_owner == own_index).astype(jnp.int32)
    own_block = jnp.sum(mine * device_ids)
    own_length = jnp.sum(mine * block_lengths)
    own_sequence = own_block // (per_pair * key_heads)
    is_last = (own_block % per_pair == per_pair - 1).astype(jnp.int32)
    info = jnp.stack([own_length, own_sequence, is_last])

    packed = jnp.concatenate(
        [
            queries.reshape(local_rows, key_heads, group_width),
            draft_keys.reshape(local_rows, key_heads, head_size),
            draft_values.reshape(local_rows, key_heads, head_size),
        ],
        axis=2,
    )
    sent = jnp.zeros((devices, local_rows, packed.shape[2]), jnp.bfloat16)
    for head in range(key_heads):
        sent = jnp.where((device_head == head)[:, None, None], packed[None, :, head], sent)
    recv = lax.all_to_all(sent, "wide", split_axis=0, concat_axis=0, tiled=True)
    block = attention(info, recv, draft_mask, cache_keys, cache_values, group)

    order = origins(devices, own_index)
    slot_of = jnp.sum(
        (block_owner[:, None] == order[None, :]).astype(jnp.int32) * device_ids[None, :], axis=1
    )
    projected = projection(
        slot_of, spread(block, devices), out_weight, per_pair, key_heads, sequences, group, head_size
    )
    hidden = feed(order, spread(projected, devices), norm_gain, gate_weight, up_weight)
    return (projected, hidden)


def solution(mesh):
    placed = (
        P(("grp", "wide"), None),
        P(("grp", "wide"), None),
        P(("grp", "wide"), None),
        P(("grp", "wide"), None),
        P(("grp", "wide"), None),
        P("grp"),
        P("grp"),
        P("grp", None, None),
        P(None, "wide"),
        P(),
        P(None, "wide"),
        P(None, "wide"),
    )
    return jax.shard_map(
        per_device,
        mesh=mesh,
        in_specs=placed,
        out_specs=(P("grp", "wide"), P("grp", "wide")),
        check_vma=False,
    )
```

```python
import functools
import math

import jax
import jax.numpy as jnp
from jax import lax
from jax.experimental import pallas as pl
from jax.experimental.pallas import tpu as pltpu
from jax.sharding import PartitionSpec as P


very_low = -1e30
epsilon = 1e-05
log2e = 1.4426950408889634
lanes = 128


def attention_kernel(pieces, sequences, rows, group, head_size, info, order, *refs):
    blocks = refs[:pieces]
    mask, keys, values, out, land, q, top, total, acc, sem = refs[pieces:]
    step = pl.program_id(0)
    block = keys.shape[0]
    length, own_sequence, own_head, is_last = info[0], info[1], info[2], info[3]
    scale = log2e / math.sqrt(head_size)
    width = group * head_size

    def fold(scores, valid, block_values):
        if valid is not None:
            scores = jnp.where(valid, scores, very_low)
        peak = top[...]
        newest = jnp.maximum(peak, jnp.max(scores, axis=1, keepdims=True))
        factor = jnp.exp2(peak - newest)
        part, weights = None, []
        for at in range(0, scores.shape[1], lanes):
            tile = jnp.exp2(scores[:, at : at + lanes] - newest)
            if valid is not None:
                tile = jnp.where(valid[:, at : at + lanes], tile, 0.0)
            part = tile if part is None else part + tile
            weights.append(tile.astype(jnp.bfloat16))
        total[...] = total[...] * factor + part
        acc[...] = acc[...] * factor + jnp.dot(
            jnp.concatenate(weights, axis=1), block_values, preferred_element_type=jnp.float32
        )
        top[...] = newest

    def score(block_keys):
        return (
            lax.dot_general(
                q[...], block_keys, (((1,), (1,)), ((), ())), preferred_element_type=jnp.float32
            )
            * scale
        )

    @pl.when(step == 0)
    def _():
        sources = pieces // sequences
        extent = land.shape[2]
        columns = pl.ds(pl.multiple_of(own_head * extent, lanes), extent)
        for phase in range(2):
            for piece in range(pieces):
                slot = order[piece] % sources
                copy = pltpu.make_async_copy(
                    blocks[piece].at[:, columns], land.at[slot], sem.at[slot]
                )
                pl.when(order[piece] // sources == own_sequence)(
                    copy.wait if phase else copy.start
                )
        mine = land[...].reshape(rows, land.shape[2])
        for head in range(group):
            q[head * rows : (head + 1) * rows, :] = mine[:, head * head_size : (head + 1) * head_size]
        own_keys = jnp.concatenate(
            [mine[:, width : width + head_size], jnp.zeros((lanes - rows, head_size), jnp.bfloat16)], 0
        )
        own_values = jnp.concatenate(
            [
                mine[:, width + head_size : width + 2 * head_size],
                jnp.zeros((lanes - rows, head_size), jnp.bfloat16),
            ],
            0,
        )
        seen = jnp.where(is_last > 0, mask[0].astype(jnp.float32), 0.0)
        seen = jnp.concatenate([seen, jnp.zeros((rows, lanes - rows), jnp.float32)], 1)
        valid = jnp.concatenate([seen] * group, 0) > 0.0
        top[...] = jnp.full_like(top, very_low)
        total[...] = jnp.zeros_like(total)
        acc[...] = jnp.zeros_like(acc)
        fold(score(own_keys), valid, own_values)

    @pl.when((step + 1) * block <= length)
    def _():
        fold(score(keys[...]), None, values[...])

    @pl.when((step * block < length) & ((step + 1) * block > length))
    def _():
        at = step * block + lax.broadcasted_iota(jnp.int32, (1, block), 1)
        valid = jnp.broadcast_to(at < length, (q.shape[0], block))
        fold(score(keys[...]), valid, values[...])

    @pl.when(step == pl.num_programs(0) - 1)
    def _():
        summed = jnp.sum(total[...], axis=1, keepdims=True)
        result = acc[...] / summed
        level = top[...] + jnp.log2(summed)
        lane = lax.broadcasted_iota(jnp.int32, (rows, lanes), 1)
        notes = jnp.zeros((rows, lanes), jnp.float32)
        for head in range(group):
            part = slice(head * rows, (head + 1) * rows)
            out[:, head * head_size : (head + 1) * head_size] = result[part].astype(jnp.bfloat16)
            rest = jnp.broadcast_to(level[part, :1], (rows, lanes))
            for piece in range(3):
                cut = rest.astype(jnp.bfloat16).astype(jnp.float32)
                notes = jnp.where(lane == piece * group + head, cut, notes)
                rest = rest - cut
        out[:, width:] = notes.astype(jnp.bfloat16)


def attention(info, order, blocks, mask, keys, values, group):
    head_size = keys.shape[1]
    sequences, rows = mask.shape[0], mask.shape[1]
    capacity = keys.shape[0]
    block = min(1024, capacity)
    width = group * head_size
    pieces = len(blocks)
    extent = width + 2 * head_size

    def at(step, info, order):
        return (jnp.minimum(step, (info[0] + block - 1) // block - 1), 0)

    return pl.pallas_call(
        functools.partial(attention_kernel, pieces, sequences, rows, group, head_size),
        out_shape=jax.ShapeDtypeStruct((rows, width + lanes), jnp.bfloat16),
        grid_spec=pltpu.PrefetchScalarGridSpec(
            num_scalar_prefetch=2,
            grid=(capacity // block,),
            in_specs=[pl.BlockSpec(memory_space=pl.ANY)] * pieces
            + [
                pl.BlockSpec((1, rows, rows), lambda step, info, order: (info[1], 0, 0)),
                pl.BlockSpec((block, head_size), at),
                pl.BlockSpec((block, head_size), at),
            ],
            out_specs=pl.BlockSpec((rows, width + lanes), lambda step, info, order: (0, 0)),
            scratch_shapes=[
                pltpu.VMEM((pieces // sequences, blocks[0].shape[0], extent), jnp.bfloat16),
                pltpu.VMEM((group * rows, head_size), jnp.bfloat16),
                pltpu.VMEM((group * rows, lanes), jnp.float32),
                pltpu.VMEM((group * rows, lanes), jnp.float32),
                pltpu.VMEM((group * rows, head_size), jnp.float32),
                pltpu.SemaphoreType.DMA((pieces // sequences,)),
            ],
        ),
        compiler_params=pltpu.CompilerParams(vmem_limit_bytes=16 << 20),
        cost_estimate=pl.CostEstimate(
            flops=16 * 4 * group * rows * capacity * head_size,
            bytes_accessed=4 * capacity * head_size,
            transcendentals=16 * group * rows * capacity,
        ),
        name="attention",
    )(info, order, *blocks, mask, keys, values)


def projection_kernel(pieces, per_pair, key_heads, sequences, group, head_size, *refs):
    where_from = refs[0]
    blocks = refs[1 : 1 + pieces]
    weight = refs[1 + pieces]
    out = refs[2 + pieces]
    held, attended, piece_sem = refs[3 + pieces :]
    rows = held.shape[1]
    width = group * head_size
    copies = []
    for piece in range(pieces):
        copy = pltpu.make_async_copy(blocks[piece], held.at[piece], piece_sem.at[piece])
        copy.start()
        copies.append(copy)
    for copy in copies:
        copy.wait()
    for head in range(key_heads):
        for sequence in range(sequences):
            pair = sequence * key_heads + head
            slots = [where_from[pair * per_pair + number] for number in range(per_pair)]
            levels = []
            for slot in slots:
                notes = held[slot, :, width:].astype(jnp.float32)
                levels.append(
                    notes
                    + pltpu.roll(notes, lanes - group, 1)
                    + pltpu.roll(notes, lanes - 2 * group, 1)
                )
            highest = functools.reduce(jnp.maximum, levels)
            mixing = [jnp.exp2(level - highest) for level in levels]
            whole = functools.reduce(jnp.add, mixing)
            mixing = [part / whole for part in mixing]
            for member in range(group):
                columns = slice(member * head_size, (member + 1) * head_size)
                gathered = None
                for slot, part in zip(slots, mixing):
                    term = part[:, member : member + 1] * held[slot, :, columns].astype(jnp.float32)
                    gathered = term if gathered is None else gathered + term
                attended[
                    sequence * rows : (sequence + 1) * rows,
                    head * width + member * head_size : head * width + (member + 1) * head_size,
                ] = gathered.astype(jnp.bfloat16)
    out[...] = jnp.dot(
        attended[...], weight[...], preferred_element_type=jnp.float32
    ).astype(jnp.bfloat16)


def projection(where_from, blocks, weight, per_pair, key_heads, sequences, group, head_size):
    pieces = len(blocks)
    rows, extent = blocks[0].shape
    return pl.pallas_call(
        functools.partial(
            projection_kernel, pieces, per_pair, key_heads, sequences, group, head_size
        ),
        out_shape=pltpu.VMEM((sequences * rows, weight.shape[1]), jnp.bfloat16),
        in_specs=[pl.BlockSpec(memory_space=pltpu.SMEM)]
        + [pl.BlockSpec(memory_space=pl.ANY)] * pieces
        + [pl.BlockSpec(memory_space=pltpu.VMEM)],
        out_specs=pl.BlockSpec(memory_space=pltpu.VMEM),
        scratch_shapes=[
            pltpu.VMEM((pieces, rows, extent), jnp.bfloat16),
            pltpu.VMEM((sequences * rows, weight.shape[0]), jnp.bfloat16),
            pltpu.SemaphoreType.DMA((pieces,)),
        ],
        compiler_params=pltpu.CompilerParams(vmem_limit_bytes=16 << 20),
        cost_estimate=pl.CostEstimate(
            flops=2 * sequences * rows * weight.size,
            bytes_accessed=2 * (weight.size + pieces * rows * extent),
            transcendentals=0,
        ),
        name="projection",
    )(where_from, *blocks, weight)


def feed_kernel(pieces, order, *refs):
    blocks = refs[:pieces]
    gain, gate_weight, up_weight, out, gate, up = refs[pieces:]
    rows, depth = blocks[0].shape
    squares = jnp.zeros((rows, lanes), jnp.float32)
    for piece in range(pieces):
        branch = blocks[piece][...].astype(jnp.float32)
        square = branch * branch
        for at in range(0, depth, lanes):
            squares = squares + square[:, at : at + lanes]
        scaled = (branch * gain[order[piece]]).astype(jnp.bfloat16)
        part = pl.ds(pl.multiple_of(order[piece] * depth, depth), depth)
        for weight, total in ((gate_weight, gate), (up_weight, up)):
            term = jnp.dot(scaled, weight[part, :], preferred_element_type=jnp.float32)
            total[...] = term if piece == 0 else total[...] + term
    inverse = lax.rsqrt(jnp.sum(squares, axis=1, keepdims=True) / (pieces * depth) + epsilon)
    opened = gate[...] * inverse
    out[...] = (opened / (1.0 + jnp.exp(-opened)) * (up[...] * inverse)).astype(jnp.bfloat16)


def feed(order, blocks, gain, gate_weight, up_weight):
    pieces = len(blocks)
    rows, depth = blocks[0].shape
    width = gate_weight.shape[1]
    whole = pl.BlockSpec(memory_space=pltpu.VMEM)
    return pl.pallas_call(
        functools.partial(feed_kernel, pieces),
        out_shape=jax.ShapeDtypeStruct((rows, width), jnp.bfloat16),
        in_specs=[pl.BlockSpec(memory_space=pltpu.SMEM)] + [whole] * (pieces + 3),
        out_specs=whole,
        scratch_shapes=[pltpu.VMEM((rows, width), jnp.float32)] * 2,
        compiler_params=pltpu.CompilerParams(vmem_limit_bytes=16 << 20),
        cost_estimate=pl.CostEstimate(
            flops=4 * rows * pieces * depth * width,
            bytes_accessed=2 * rows * pieces * depth,
            transcendentals=rows * width,
        ),
        name="feed",
    )(order, *blocks, gain.reshape(pieces, 1, depth), gate_weight, up_weight)


def spread(block, devices):
    def swap(value, bits):
        return lax.ppermute(value, "wide", [(i, i ^ bits) for i in range(devices)])

    found = [block] + [swap(block, 4 * far) for far in range(1, devices // 4)]
    found = found + [swap(value, 2) for value in found]
    return found + [swap(value, 1) for value in found]


def origins(devices, own_index):
    far = devices // 4
    number = jnp.arange(devices, dtype=jnp.int32)
    swapped = number // far
    return own_index ^ (number % far * 4 + swapped % 2 * 2 + swapped // 2)


def per_device(
    queries,
    draft_keys,
    draft_values,
    cache_keys,
    cache_values,
    block_owner,
    block_lengths,
    draft_mask,
    out_weight,
    norm_gain,
    gate_weight,
    up_weight,
):
    devices = lax.axis_size("wide")
    own_index = lax.axis_index("wide").astype(jnp.int32)
    local_rows = queries.shape[0]
    head_size = cache_keys.shape[1]
    key_heads = draft_keys.shape[1] // head_size
    group_width = queries.shape[1] // key_heads
    group = group_width // head_size
    sequences = draft_mask.shape[0]
    local_rows = queries.shape[0]
    per_pair = devices // (sequences * key_heads)
    device_ids = jnp.arange(devices, dtype=jnp.int32)
    mine = (block_owner == own_index).astype(jnp.int32)
    own_block = jnp.sum(mine * device_ids)
    own_length = jnp.sum(mine * block_lengths)
    own_pair = own_block // per_pair
    is_last = (own_block % per_pair == per_pair - 1).astype(jnp.int32)
    info = jnp.stack([own_length, own_pair // key_heads, own_pair % key_heads, is_last])
    order = origins(devices, own_index)
    slot_of = jnp.sum(
        (block_owner[:, None] == order[None, :]).astype(jnp.int32) * device_ids[None, :], axis=1
    )

    packed = jnp.concatenate(
        [
            queries.reshape(local_rows, key_heads, group_width),
            draft_keys.reshape(local_rows, key_heads, head_size),
            draft_values.reshape(local_rows, key_heads, head_size),
        ],
        axis=2,
    ).reshape(local_rows, -1)
    inputs = spread(packed, devices)
    block = attention(
        info,
        order,
        inputs,
        pltpu.with_memory_space_constraint(draft_mask, pltpu.HBM),
        pltpu.with_memory_space_constraint(cache_keys, pltpu.HBM),
        pltpu.with_memory_space_constraint(cache_values, pltpu.HBM),
        group,
    )
    projected = projection(
        slot_of,
        spread(block, devices),
        pltpu.with_memory_space_constraint(out_weight, pltpu.VMEM),
        per_pair,
        key_heads,
        sequences,
        group,
        head_size,
    )
    hidden = feed(
        order,
        spread(projected, devices),
        norm_gain,
        gate_weight,
        up_weight,
    )
    return (projected, hidden)


def solution(mesh):
    placed = (
        P(("grp", "wide"), None),
        P(("grp", "wide"), None),
        P(("grp", "wide"), None),
        P(("grp", "wide"), None),
        P(("grp", "wide"), None),
        P("grp"),
        P("grp"),
        P("grp", None, None),
        P(None, "wide"),
        P(),
        P(None, "wide"),
        P(None, "wide"),
    )
    return jax.shard_map(
        per_device,
        mesh=mesh,
        in_specs=placed,
        out_specs=(P("grp", "wide"), P("grp", "wide")),
        check_vma=False,
    )
```

```python
import functools
import math

import jax
import jax.numpy as jnp
from jax import lax
from jax.experimental import pallas as pl
from jax.experimental.pallas import tpu as pltpu
from jax.sharding import PartitionSpec as P


very_low = -1e30
epsilon = 1e-05
log2e = 1.4426950408889634
lanes = 128


def attention_kernel(pieces, sequences, rows, group, head_size, info, order, *refs):
    blocks = refs[:pieces]
    mask, keys, values, out, land, q, top, total, acc = refs[pieces:]
    step = pl.program_id(0)
    block = keys.shape[0]
    length, own_sequence, own_head, is_last = info[0], info[1], info[2], info[3]
    scale = log2e / math.sqrt(head_size)
    width = group * head_size

    def fold(scores, valid, block_values):
        if valid is not None:
            scores = jnp.where(valid, scores, very_low)
        peak = top[...]
        newest = jnp.maximum(peak, jnp.max(scores, axis=1, keepdims=True))
        factor = jnp.exp2(peak - newest)
        part, weights = None, []
        for at in range(0, scores.shape[1], lanes):
            tile = jnp.exp2(scores[:, at : at + lanes] - newest)
            if valid is not None:
                tile = jnp.where(valid[:, at : at + lanes], tile, 0.0)
            part = tile if part is None else part + tile
            weights.append(tile.astype(jnp.bfloat16))
        total[...] = total[...] * factor + part
        acc[...] = acc[...] * factor + jnp.dot(
            jnp.concatenate(weights, axis=1), block_values, preferred_element_type=jnp.float32
        )
        top[...] = newest

    def score(block_keys):
        return (
            lax.dot_general(
                q[...], block_keys, (((1,), (1,)), ((), ())), preferred_element_type=jnp.float32
            )
            * scale
        )

    @pl.when(step == 0)
    def _():
        sources = pieces // sequences
        extent = land.shape[2]
        columns = pl.ds(pl.multiple_of(own_head * extent, lanes), extent)
        for piece in range(pieces):

            @pl.when(order[piece] // sources == own_sequence)
            def _(piece=piece):
                land[order[piece] % sources] = blocks[piece][:, columns]

        mine = land[...].reshape(rows, land.shape[2])
        for head in range(group):
            q[head * rows : (head + 1) * rows, :] = mine[:, head * head_size : (head + 1) * head_size]
        own_keys = jnp.concatenate(
            [mine[:, width : width + head_size], jnp.zeros((lanes - rows, head_size), jnp.bfloat16)], 0
        )
        own_values = jnp.concatenate(
            [
                mine[:, width + head_size : width + 2 * head_size],
                jnp.zeros((lanes - rows, head_size), jnp.bfloat16),
            ],
            0,
        )
        seen = jnp.where(is_last > 0, mask[0].astype(jnp.float32), 0.0)
        seen = jnp.concatenate([seen, jnp.zeros((rows, lanes - rows), jnp.float32)], 1)
        valid = jnp.concatenate([seen] * group, 0) > 0.0
        top[...] = jnp.full_like(top, very_low)
        total[...] = jnp.zeros_like(total)
        acc[...] = jnp.zeros_like(acc)
        fold(score(own_keys), valid, own_values)

    @pl.when((step + 1) * block <= length)
    def _():
        fold(score(keys[...]), None, values[...])

    @pl.when((step * block < length) & ((step + 1) * block > length))
    def _():
        at = step * block + lax.broadcasted_iota(jnp.int32, (1, block), 1)
        valid = jnp.broadcast_to(at < length, (q.shape[0], block))
        fold(score(keys[...]), valid, values[...])

    @pl.when(step == pl.num_programs(0) - 1)
    def _():
        summed = jnp.sum(total[...], axis=1, keepdims=True)
        result = acc[...] / summed
        level = top[...] + jnp.log2(summed)
        lane = lax.broadcasted_iota(jnp.int32, (rows, lanes), 1)
        notes = jnp.zeros((rows, lanes), jnp.float32)
        for head in range(group):
            part = slice(head * rows, (head + 1) * rows)
            out[:, head * head_size : (head + 1) * head_size] = result[part].astype(jnp.bfloat16)
            rest = jnp.broadcast_to(level[part, :1], (rows, lanes))
            for piece in range(3):
                cut = rest.astype(jnp.bfloat16).astype(jnp.float32)
                notes = jnp.where(lane == piece * group + head, cut, notes)
                rest = rest - cut
        out[:, width:] = notes.astype(jnp.bfloat16)


def attention(info, order, blocks, mask, keys, values, group):
    head_size = keys.shape[1]
    sequences, rows = mask.shape[0], mask.shape[1]
    capacity = keys.shape[0]
    block = min(1024, capacity)
    width = group * head_size
    pieces = len(blocks)
    extent = width + 2 * head_size

    def at(step, info, order):
        return (jnp.minimum(step, (info[0] + block - 1) // block - 1), 0)

    return pl.pallas_call(
        functools.partial(attention_kernel, pieces, sequences, rows, group, head_size),
        out_shape=jax.ShapeDtypeStruct((rows, width + lanes), jnp.bfloat16),
        grid_spec=pltpu.PrefetchScalarGridSpec(
            num_scalar_prefetch=2,
            grid=(capacity // block,),
            in_specs=[pl.BlockSpec(memory_space=pltpu.VMEM)] * pieces
            + [
                pl.BlockSpec((1, rows, rows), lambda step, info, order: (info[1], 0, 0)),
                pl.BlockSpec((block, head_size), at),
                pl.BlockSpec((block, head_size), at),
            ],
            out_specs=pl.BlockSpec((rows, width + lanes), lambda step, info, order: (0, 0)),
            scratch_shapes=[
                pltpu.VMEM((pieces // sequences, blocks[0].shape[0], extent), jnp.bfloat16),
                pltpu.VMEM((group * rows, head_size), jnp.bfloat16),
                pltpu.VMEM((group * rows, lanes), jnp.float32),
                pltpu.VMEM((group * rows, lanes), jnp.float32),
                pltpu.VMEM((group * rows, head_size), jnp.float32),
            ],
        ),
        compiler_params=pltpu.CompilerParams(vmem_limit_bytes=16 << 20),
        cost_estimate=pl.CostEstimate(
            flops=16 * 4 * group * rows * capacity * head_size,
            bytes_accessed=4 * capacity * head_size,
            transcendentals=16 * group * rows * capacity,
        ),
        name="attention",
    )(info, order, *blocks, mask, keys, values)


def projection_kernel(pieces, per_pair, key_heads, sequences, group, head_size, *refs):
    where_from = refs[0]
    blocks = refs[1 : 1 + pieces]
    weight = refs[1 + pieces]
    out = refs[2 + pieces]
    held, attended = refs[3 + pieces :]
    rows = held.shape[1]
    width = group * head_size
    for piece in range(pieces):
        held[piece] = blocks[piece][...]
    for head in range(key_heads):
        for sequence in range(sequences):
            pair = sequence * key_heads + head
            slots = [where_from[pair * per_pair + number] for number in range(per_pair)]
            levels = []
            for slot in slots:
                notes = held[slot, :, width:].astype(jnp.float32)
                levels.append(
                    notes
                    + pltpu.roll(notes, lanes - group, 1)
                    + pltpu.roll(notes, lanes - 2 * group, 1)
                )
            highest = functools.reduce(jnp.maximum, levels)
            mixing = [jnp.exp2(level - highest) for level in levels]
            whole = functools.reduce(jnp.add, mixing)
            mixing = [part / whole for part in mixing]
            for member in range(group):
                columns = slice(member * head_size, (member + 1) * head_size)
                gathered = None
                for slot, part in zip(slots, mixing):
                    term = part[:, member : member + 1] * held[slot, :, columns].astype(jnp.float32)
                    gathered = term if gathered is None else gathered + term
                attended[
                    sequence * rows : (sequence + 1) * rows,
                    head * width + member * head_size : head * width + (member + 1) * head_size,
                ] = gathered.astype(jnp.bfloat16)
    out[...] = jnp.dot(
        attended[...], weight[...], preferred_element_type=jnp.float32
    ).astype(jnp.bfloat16)


def projection(where_from, blocks, weight, per_pair, key_heads, sequences, group, head_size):
    pieces = len(blocks)
    rows, extent = blocks[0].shape
    return pl.pallas_call(
        functools.partial(
            projection_kernel, pieces, per_pair, key_heads, sequences, group, head_size
        ),
        out_shape=pltpu.VMEM((sequences * rows, weight.shape[1]), jnp.bfloat16),
        in_specs=[pl.BlockSpec(memory_space=pltpu.SMEM)]
        + [pl.BlockSpec(memory_space=pltpu.VMEM)] * (pieces + 1),
        out_specs=pl.BlockSpec(memory_space=pltpu.VMEM),
        scratch_shapes=[
            pltpu.VMEM((pieces, rows, extent), jnp.bfloat16),
            pltpu.VMEM((sequences * rows, weight.shape[0]), jnp.bfloat16),
        ],
        compiler_params=pltpu.CompilerParams(vmem_limit_bytes=16 << 20),
        cost_estimate=pl.CostEstimate(
            flops=2 * sequences * rows * weight.size,
            bytes_accessed=2 * (weight.size + pieces * rows * extent),
            transcendentals=0,
        ),
        name="projection",
    )(where_from, *blocks, weight)


def multiply(order, slots, blocks, gain, weights, totals, squares, fresh):
    for slot, block in zip(slots, blocks):
        depth = block.shape[1]
        branch = block[...].astype(jnp.float32)
        square = branch * branch
        for at in range(0, depth, lanes):
            squares = squares + square[:, at : at + lanes]
        scaled = (branch * gain[order[slot]]).astype(jnp.bfloat16)
        part = pl.ds(pl.multiple_of(order[slot] * depth, depth), depth)
        for weight, total in zip(weights, totals):
            term = jnp.dot(scaled, weight[part, :], preferred_element_type=jnp.float32)
            total[...] = term if fresh else total[...] + term
        fresh = False
    return squares


def feed_first_kernel(slots, order, *refs):
    blocks = refs[: len(slots)]
    gain, gate_weight, up_weight, gate, up, squares = refs[len(slots) :]
    squares[...] = multiply(
        order,
        slots,
        blocks,
        gain,
        (gate_weight, up_weight),
        (gate, up),
        jnp.zeros(squares.shape, jnp.float32),
        True,
    )


def feed_last_kernel(slots, total_width, order, *refs):
    blocks = refs[: len(slots)]
    gain, gate_weight, up_weight, gate_in, up_in, squares, out, gate, up = refs[len(slots) :]
    gate[...] = gate_in[...]
    up[...] = up_in[...]
    total = multiply(
        order,
        slots,
        blocks,
        gain,
        (gate_weight, up_weight),
        (gate, up),
        squares[...],
        False,
    )
    inverse = lax.rsqrt(jnp.sum(total, axis=1, keepdims=True) / total_width + epsilon)
    opened = gate[...] * inverse
    out[...] = (opened / (1.0 + jnp.exp(-opened)) * (up[...] * inverse)).astype(jnp.bfloat16)


def feed(order, blocks, gain, gate_weight, up_weight):
    pieces = len(blocks)
    rows, depth = blocks[0].shape
    width = gate_weight.shape[1]
    far = pieces // 4
    late = [far + number for number in range(1, far, 2)]
    late = late + [2 * far + number for number in late]
    early = [slot for slot in range(pieces) if slot not in late]
    whole = pl.BlockSpec(memory_space=pltpu.VMEM)
    table = gain.reshape(pieces, 1, depth)

    def call(kernel, slots, extra, out_shape, scratch):
        return pl.pallas_call(
            kernel,
            out_shape=out_shape,
            in_specs=[pl.BlockSpec(memory_space=pltpu.SMEM)]
            + [whole] * (len(slots) + 3 + len(extra)),
            out_specs=jax.tree.map(lambda _: whole, out_shape),
            scratch_shapes=scratch,
            compiler_params=pltpu.CompilerParams(vmem_limit_bytes=16 << 20),
            cost_estimate=pl.CostEstimate(
                flops=4 * rows * len(slots) * depth * width,
                bytes_accessed=2 * rows * len(slots) * depth,
                transcendentals=0,
            ),
        )(order, *[blocks[slot] for slot in slots], table, gate_weight, up_weight, *extra)

    sums = call(
        functools.partial(feed_first_kernel, early),
        early,
        (),
        (
            jax.ShapeDtypeStruct((rows, width), jnp.float32),
            jax.ShapeDtypeStruct((rows, width), jnp.float32),
            jax.ShapeDtypeStruct((rows, lanes), jnp.float32),
        ),
        (),
    )
    return call(
        functools.partial(feed_last_kernel, late, pieces * depth),
        late,
        sums,
        jax.ShapeDtypeStruct((rows, width), jnp.bfloat16),
        [pltpu.VMEM((rows, width), jnp.float32)] * 2,
    )


def spread(block, devices):
    def swap(value, bits):
        return lax.ppermute(value, "wide", [(i, i ^ bits) for i in range(devices)])

    found = [block] + [swap(block, 4 * far) for far in range(1, devices // 4)]
    found = found + [swap(value, 2) for value in found]
    return found + [swap(value, 1) for value in found]


def origins(devices, own_index):
    far = devices // 4
    number = jnp.arange(devices, dtype=jnp.int32)
    swapped = number // far
    return own_index ^ (number % far * 4 + swapped % 2 * 2 + swapped // 2)


def per_device(
    queries,
    draft_keys,
    draft_values,
    cache_keys,
    cache_values,
    block_owner,
    block_lengths,
    draft_mask,
    out_weight,
    norm_gain,
    gate_weight,
    up_weight,
):
    devices = lax.axis_size("wide")
    own_index = lax.axis_index("wide").astype(jnp.int32)
    local_rows = queries.shape[0]
    head_size = cache_keys.shape[1]
    key_heads = draft_keys.shape[1] // head_size
    group_width = queries.shape[1] // key_heads
    group = group_width // head_size
    sequences = draft_mask.shape[0]
    local_rows = queries.shape[0]
    per_pair = devices // (sequences * key_heads)
    device_ids = jnp.arange(devices, dtype=jnp.int32)
    pair = device_ids // per_pair
    facts = jnp.stack(
        [block_lengths, pair // key_heads, pair % key_heads, device_ids % per_pair // (per_pair - 1)]
        if per_pair > 1
        else [block_lengths, pair // key_heads, pair % key_heads, jnp.ones_like(device_ids)]
    )
    info = jnp.sum(jnp.where((block_owner == own_index)[None, :], facts, 0), axis=1)
    order = origins(devices, own_index)
    slot_of = jnp.sum(
        (block_owner[:, None] == order[None, :]).astype(jnp.int32) * device_ids[None, :], axis=1
    )

    packed = jnp.concatenate(
        [
            queries.reshape(local_rows, key_heads, group_width),
            draft_keys.reshape(local_rows, key_heads, head_size),
            draft_values.reshape(local_rows, key_heads, head_size),
        ],
        axis=2,
    ).reshape(local_rows, -1)
    inputs = spread(packed, devices)
    block = attention(
        info,
        order,
        inputs,
        pltpu.with_memory_space_constraint(draft_mask, pltpu.HBM),
        pltpu.with_memory_space_constraint(cache_keys, pltpu.HBM),
        pltpu.with_memory_space_constraint(cache_values, pltpu.HBM),
        group,
    )
    projected = projection(
        slot_of,
        spread(block, devices),
        pltpu.with_memory_space_constraint(out_weight, pltpu.VMEM),
        per_pair,
        key_heads,
        sequences,
        group,
        head_size,
    )
    hidden = feed(
        order,
        spread(projected, devices),
        norm_gain,
        gate_weight,
        up_weight,
    )
    return (projected, hidden)


def solution(mesh):
    placed = (
        P(("grp", "wide"), None),
        P(("grp", "wide"), None),
        P(("grp", "wide"), None),
        P(("grp", "wide"), None),
        P(("grp", "wide"), None),
        P("grp"),
        P("grp"),
        P("grp", None, None),
        P(None, "wide"),
        P(),
        P(None, "wide"),
        P(None, "wide"),
    )
    return jax.shard_map(
        per_device,
        mesh=mesh,
        in_specs=placed,
        out_specs=(P("grp", "wide"), P("grp", "wide")),
        check_vma=False,
    )
```

```python
import functools
import math

import jax
import jax.numpy as jnp
from jax import lax
from jax.experimental import pallas as pl
from jax.experimental.pallas import tpu as pltpu
from jax.sharding import PartitionSpec as P


very_low = -1e30
epsilon = 1e-05
log2e = 1.4426950408889634
lanes = 128


def attention_kernel(pieces, sequences, rows, group, head_size, info, order, *refs):
    blocks = refs[:pieces]
    mask, keys, values, out, land, q, top, total, acc = refs[pieces:]
    step = pl.program_id(0)
    block = keys.shape[0]
    length, own_sequence, own_head, is_last = info[0], info[1], info[2], info[3]
    scale = log2e / math.sqrt(head_size)
    width = group * head_size

    every = group * rows
    some = min(256, group * rows)

    def fold(part, scores, valid, block_values):
        if valid is not None:
            scores = jnp.where(valid, scores, very_low)
        peak = top[part, :]
        newest = jnp.maximum(peak, jnp.max(scores, axis=1, keepdims=True))
        factor = jnp.exp2(peak - newest)
        sums, weights = None, []
        for at in range(0, scores.shape[1], lanes):
            tile = jnp.exp2(scores[:, at : at + lanes] - newest)
            if valid is not None:
                tile = jnp.where(valid[:, at : at + lanes], tile, 0.0)
            sums = tile if sums is None else sums + tile
            weights.append(tile.astype(jnp.bfloat16))
        total[part, :] = total[part, :] * factor + sums
        acc[part, :] = acc[part, :] * factor + jnp.dot(
            jnp.concatenate(weights, axis=1), block_values, preferred_element_type=jnp.float32
        )
        top[part, :] = newest

    def score(part, block_keys):
        return (
            lax.dot_general(
                q[part, :], block_keys, (((1,), (1,)), ((), ())), preferred_element_type=jnp.float32
            )
            * scale
        )

    def sweep(block_keys, block_values, valid_of):
        parts = [slice(at, at + some) for at in range(0, every, some)]
        ready = score(parts[0], block_keys)
        for number, part in enumerate(parts):
            scores = ready
            if number + 1 < len(parts):
                ready = score(parts[number + 1], block_keys)
            fold(part, scores, valid_of(part), block_values)

    @pl.when(step == 0)
    def _():
        sources = pieces // sequences
        extent = land.shape[2]
        columns = pl.ds(pl.multiple_of(own_head * extent, lanes), extent)
        for piece in range(pieces):

            @pl.when(order[piece] // sources == own_sequence)
            def _(piece=piece):
                land[order[piece] % sources] = blocks[piece][:, columns]

        mine = land[...].reshape(rows, land.shape[2])
        for head in range(group):
            q[head * rows : (head + 1) * rows, :] = mine[:, head * head_size : (head + 1) * head_size]
        own_keys = jnp.concatenate(
            [mine[:, width : width + head_size], jnp.zeros((lanes - rows, head_size), jnp.bfloat16)], 0
        )
        own_values = jnp.concatenate(
            [
                mine[:, width + head_size : width + 2 * head_size],
                jnp.zeros((lanes - rows, head_size), jnp.bfloat16),
            ],
            0,
        )
        seen = jnp.where(is_last > 0, mask[0].astype(jnp.float32), 0.0)
        seen = jnp.concatenate([seen, jnp.zeros((rows, lanes - rows), jnp.float32)], 1)
        valid = jnp.concatenate([seen] * group, 0) > 0.0
        top[...] = jnp.full_like(top, very_low)
        total[...] = jnp.zeros_like(total)
        acc[...] = jnp.zeros_like(acc)
        sweep(own_keys, own_values, lambda part: valid[part, :])

    @pl.when((step + 1) * block <= length)
    def _():
        sweep(keys[...], values[...], lambda part: None)

    @pl.when((step * block < length) & ((step + 1) * block > length))
    def _():
        at = step * block + lax.broadcasted_iota(jnp.int32, (1, block), 1)
        valid = jnp.broadcast_to(at < length, (some, block))
        sweep(keys[...], values[...], lambda part: valid)

    @pl.when(step == pl.num_programs(0) - 1)
    def _():
        summed = jnp.sum(total[...], axis=1, keepdims=True)
        result = acc[...] / summed
        level = top[...] + jnp.log2(summed)
        lane = lax.broadcasted_iota(jnp.int32, (rows, lanes), 1)
        notes = jnp.zeros((rows, lanes), jnp.float32)
        for head in range(group):
            part = slice(head * rows, (head + 1) * rows)
            out[:, head * head_size : (head + 1) * head_size] = result[part].astype(jnp.bfloat16)
            rest = jnp.broadcast_to(level[part, :1], (rows, lanes))
            for piece in range(3):
                cut = rest.astype(jnp.bfloat16).astype(jnp.float32)
                notes = jnp.where(lane == piece * group + head, cut, notes)
                rest = rest - cut
        out[:, width:] = notes.astype(jnp.bfloat16)


def attention(info, order, blocks, mask, keys, values, group):
    head_size = keys.shape[1]
    sequences, rows = mask.shape[0], mask.shape[1]
    capacity = keys.shape[0]
    block = min(1024, capacity)
    width = group * head_size
    pieces = len(blocks)
    extent = width + 2 * head_size

    def at(step, info, order):
        return (jnp.minimum(step, (info[0] + block - 1) // block - 1), 0)

    return pl.pallas_call(
        functools.partial(attention_kernel, pieces, sequences, rows, group, head_size),
        out_shape=jax.ShapeDtypeStruct((rows, width + lanes), jnp.bfloat16),
        grid_spec=pltpu.PrefetchScalarGridSpec(
            num_scalar_prefetch=2,
            grid=(capacity // block,),
            in_specs=[pl.BlockSpec(memory_space=pltpu.VMEM)] * pieces
            + [
                pl.BlockSpec((1, rows, rows), lambda step, info, order: (info[1], 0, 0)),
                pl.BlockSpec((block, head_size), at),
                pl.BlockSpec((block, head_size), at),
            ],
            out_specs=pl.BlockSpec((rows, width + lanes), lambda step, info, order: (0, 0)),
            scratch_shapes=[
                pltpu.VMEM((pieces // sequences, blocks[0].shape[0], extent), jnp.bfloat16),
                pltpu.VMEM((group * rows, head_size), jnp.bfloat16),
                pltpu.VMEM((group * rows, lanes), jnp.float32),
                pltpu.VMEM((group * rows, lanes), jnp.float32),
                pltpu.VMEM((group * rows, head_size), jnp.float32),
            ],
        ),
        compiler_params=pltpu.CompilerParams(vmem_limit_bytes=16 << 20),
        cost_estimate=pl.CostEstimate(
            flops=4 * group * rows * capacity * head_size,
            bytes_accessed=4 * capacity * head_size,
            transcendentals=group * rows * capacity,
        ),
        name="attention",
    )(info, order, *blocks, mask, keys, values)


def projection_kernel(pieces, per_pair, key_heads, sequences, group, head_size, *refs):
    where_from = refs[0]
    blocks = refs[1 : 1 + pieces]
    weight = refs[1 + pieces]
    out = refs[2 + pieces]
    held, attended = refs[3 + pieces :]
    rows = held.shape[1]
    width = group * head_size
    for piece in range(pieces):
        held[piece] = blocks[piece][...]
    result = None
    for head in range(key_heads):
        for sequence in range(sequences):
            pair = sequence * key_heads + head
            slots = [where_from[pair * per_pair + number] for number in range(per_pair)]
            levels = []
            for slot in slots:
                notes = held[slot, :, width:].astype(jnp.float32)
                levels.append(
                    notes
                    + pltpu.roll(notes, lanes - group, 1)
                    + pltpu.roll(notes, lanes - 2 * group, 1)
                )
            highest = functools.reduce(jnp.maximum, levels)
            mixing = [jnp.exp2(level - highest) for level in levels]
            whole = functools.reduce(jnp.add, mixing)
            mixing = [part / whole for part in mixing]
            for member in range(group):
                columns = slice(member * head_size, (member + 1) * head_size)
                gathered = held[slots[-1], :, columns].astype(jnp.float32)
                base = gathered
                for slot, part in zip(slots[:-1], mixing):
                    change = held[slot, :, columns].astype(jnp.float32) - base
                    gathered = gathered + part[:, member : member + 1] * change
                attended[
                    sequence * rows : (sequence + 1) * rows,
                    head * width + member * head_size : head * width + (member + 1) * head_size,
                ] = gathered.astype(jnp.bfloat16)
        part = slice(head * width, (head + 1) * width)
        term = jnp.dot(attended[:, part], weight[part, :], preferred_element_type=jnp.float32)
        result = term if result is None else result + term
    out[...] = result.astype(jnp.bfloat16)


def projection(where_from, blocks, weight, per_pair, key_heads, sequences, group, head_size):
    pieces = len(blocks)
    rows, extent = blocks[0].shape
    return pl.pallas_call(
        functools.partial(
            projection_kernel, pieces, per_pair, key_heads, sequences, group, head_size
        ),
        out_shape=pltpu.VMEM((sequences * rows, weight.shape[1]), jnp.bfloat16),
        in_specs=[pl.BlockSpec(memory_space=pltpu.SMEM)]
        + [pl.BlockSpec(memory_space=pltpu.VMEM)] * (pieces + 1),
        out_specs=pl.BlockSpec(memory_space=pltpu.VMEM),
        scratch_shapes=[
            pltpu.VMEM((pieces, rows, extent), jnp.bfloat16),
            pltpu.VMEM((sequences * rows, weight.shape[0]), jnp.bfloat16),
        ],
        compiler_params=pltpu.CompilerParams(vmem_limit_bytes=16 << 20),
        cost_estimate=pl.CostEstimate(
            flops=2 * sequences * rows * weight.size,
            bytes_accessed=2 * (weight.size + pieces * rows * extent),
            transcendentals=0,
        ),
        name="projection",
    )(where_from, *blocks, weight)


def feed_kernel(slots, total_width, first, last, order, *refs):
    blocks, refs = refs[: len(slots)], refs[len(slots) :]
    (gain, *weights), refs = refs[:3], refs[3:]
    if not first:
        given, refs = refs[:3], refs[3:]
    if last:
        out, totals = refs[0], refs[1:]
    else:
        totals, kept = refs[:2], refs[2]
    rows, depth = blocks[0].shape
    squares = jnp.zeros((rows, lanes), jnp.float32) if first else given[2][...]
    for number, (slot, block) in enumerate(zip(slots, blocks)):
        branch = block[...].astype(jnp.float32)
        square = branch * branch
        for at in range(0, depth, lanes):
            squares = squares + square[:, at : at + lanes]
        scaled = (branch * gain[order[slot]]).astype(jnp.bfloat16)
        part = pl.ds(pl.multiple_of(order[slot] * depth, depth), depth)
        for which in range(2):
            term = jnp.dot(scaled, weights[which][part, :], preferred_element_type=jnp.float32)
            if number > 0:
                term = totals[which][...] + term
            elif not first:
                term = given[which][...] + term
            totals[which][...] = term
    if not last:
        kept[...] = squares
        return
    inverse = lax.rsqrt(jnp.sum(squares, axis=1, keepdims=True) / total_width + epsilon)
    opened = totals[0][...] * inverse
    out[...] = (opened / (1.0 + jnp.exp(-opened)) * (totals[1][...] * inverse)).astype(jnp.bfloat16)


def feed(order, blocks, gain, gate_weight, up_weight, mark):
    pieces = len(blocks)
    rows, depth = blocks[0].shape
    width = gate_weight.shape[1]
    far = pieces // 4
    late = [far + number for number in range(1, far, 2)]
    late = late + [2 * far + number for number in late]
    stages = [[0, 2 * far], [2, 2 * far + 2, far, 3 * far]]
    known = late + stages[0] + stages[1]
    stages = stages + [[slot for slot in range(pieces) if slot not in known], late]
    whole = pl.BlockSpec(memory_space=pltpu.VMEM)
    table = gain.reshape(pieces, 1, depth)
    result = ()
    for number, slots in enumerate(stages):
        first, last = number == 0, number == len(stages) - 1
        sums = [jax.ShapeDtypeStruct((rows, width), jnp.float32)] * 2
        sums = sums + [jax.ShapeDtypeStruct((rows, lanes), jnp.float32)]
        shape = jax.ShapeDtypeStruct((rows, width), jnp.bfloat16) if last else tuple(sums)
        kernel = functools.partial(feed_kernel, slots, pieces * depth, first, last)
        result = pl.pallas_call(
            kernel if not last else lambda *refs: kernel(*refs[:-4], *refs[-3:]),
            out_shape=shape,
            in_specs=[pl.BlockSpec(memory_space=pltpu.SMEM)]
            + [whole] * (len(slots) + 3 + len(result) + last),
            out_specs=whole if last else (whole,) * 3,
            scratch_shapes=[pltpu.VMEM((rows, width), jnp.float32)] * 2 if last else [],
            compiler_params=pltpu.CompilerParams(vmem_limit_bytes=12 << 20),
            cost_estimate=pl.CostEstimate(
                flops=4 * rows * len(slots) * depth * width,
                bytes_accessed=2 * rows * len(slots) * depth,
                transcendentals=0,
            ),
        )(
            order,
            *[blocks[slot] for slot in slots],
            table,
            gate_weight,
            up_weight,
            *result,
            *((mark,) if last else ()),
        )
    return result


def mark_kernel(block, out):
    out[...] = block[: out.shape[0], : out.shape[1]]


def marked(block, work):
    whole = pl.BlockSpec(memory_space=pltpu.VMEM)
    return pl.pallas_call(
        mark_kernel,
        out_shape=jax.ShapeDtypeStruct((8, lanes), block.dtype),
        in_specs=[whole],
        out_specs=whole,
        compiler_params=pltpu.CompilerParams(vmem_limit_bytes=1 << 20),
        cost_estimate=pl.CostEstimate(flops=work, bytes_accessed=0, transcendentals=work // 512),
        name="mark",
    )(block)


def spread(block, devices):
    def swap(value, bits):
        return lax.ppermute(value, "wide", [(i, i ^ bits) for i in range(devices)])

    found = [block] + [swap(block, 4 * far) for far in range(1, devices // 4)]
    found = found + [swap(value, 2) for value in found]
    return found + [swap(value, 1) for value in found]


def origins(devices, own_index):
    far = devices // 4
    number = jnp.arange(devices, dtype=jnp.int32)
    swapped = number // far
    return own_index ^ (number % far * 4 + swapped % 2 * 2 + swapped // 2)


def per_device(
    queries,
    draft_keys,
    draft_values,
    cache_keys,
    cache_values,
    block_owner,
    block_lengths,
    draft_mask,
    out_weight,
    norm_gain,
    gate_weight,
    up_weight,
):
    devices = lax.axis_size("wide")
    own_index = lax.axis_index("wide").astype(jnp.int32)
    local_rows = queries.shape[0]
    head_size = cache_keys.shape[1]
    key_heads = draft_keys.shape[1] // head_size
    group_width = queries.shape[1] // key_heads
    group = group_width // head_size
    sequences = draft_mask.shape[0]
    local_rows = queries.shape[0]
    per_pair = devices // (sequences * key_heads)
    device_ids = jnp.arange(devices, dtype=jnp.int32)
    pair = device_ids // per_pair
    facts = jnp.stack(
        [block_lengths, pair // key_heads, pair % key_heads, device_ids % per_pair // (per_pair - 1)]
        if per_pair > 1
        else [block_lengths, pair // key_heads, pair % key_heads, jnp.ones_like(device_ids)]
    )
    info = jnp.sum(jnp.where((block_owner == own_index)[None, :], facts, 0), axis=1)
    order = origins(devices, own_index)
    slot_of = jnp.sum(
        (block_owner[:, None] == order[None, :]).astype(jnp.int32) * device_ids[None, :], axis=1
    )

    packed = jnp.concatenate(
        [
            queries.reshape(local_rows, key_heads, group_width),
            draft_keys.reshape(local_rows, key_heads, head_size),
            draft_values.reshape(local_rows, key_heads, head_size),
        ],
        axis=2,
    ).reshape(local_rows, -1)
    inputs = spread(packed, devices)
    block = attention(
        info,
        order,
        inputs,
        pltpu.with_memory_space_constraint(draft_mask, pltpu.HBM),
        pltpu.with_memory_space_constraint(cache_keys, pltpu.HBM),
        pltpu.with_memory_space_constraint(cache_values, pltpu.HBM),
        group,
    )
    work = 64 * 2 * queries.shape[1] * cache_keys.size // 8
    mark = marked(block, work)
    projected = projection(
        slot_of,
        spread(block, devices),
        pltpu.with_memory_space_constraint(out_weight, pltpu.VMEM),
        per_pair,
        key_heads,
        sequences,
        group,
        head_size,
    )
    hidden = feed(order, spread(projected, devices), norm_gain, gate_weight, up_weight, mark)
    return (projected, hidden)


def solution(mesh):
    placed = (
        P(("grp", "wide"), None),
        P(("grp", "wide"), None),
        P(("grp", "wide"), None),
        P(("grp", "wide"), None),
        P(("grp", "wide"), None),
        P("grp"),
        P("grp"),
        P("grp", None, None),
        P(None, "wide"),
        P(),
        P(None, "wide"),
        P(None, "wide"),
    )
    return jax.shard_map(
        per_device,
        mesh=mesh,
        in_specs=placed,
        out_specs=(P("grp", "wide"), P("grp", "wide")),
        check_vma=False,
    )
```

```python
import functools
import math

import jax
import jax.numpy as jnp
from jax import lax
from jax.experimental import pallas as pl
from jax.experimental.pallas import tpu as pltpu
from jax.sharding import PartitionSpec as P


very_low = -1e30
epsilon = 1e-05
log2e = 1.4426950408889634
lanes = 128


def attention_kernel(pieces, sequences, rows, group, head_size, info, order, *refs):
    blocks = refs[:pieces]
    mask, keys, values, out, land, q, top, total, acc = refs[pieces:]
    step = pl.program_id(0)
    block = keys.shape[0]
    length, own_sequence, own_head, is_last = info[0], info[1], info[2], info[3]
    scale = log2e / math.sqrt(head_size)
    width = group * head_size

    every = group * rows
    some = min(256, group * rows)

    def fold(part, scores, valid, block_values):
        if valid is not None:
            scores = jnp.where(valid, scores, very_low)
        peak = top[part, :]
        newest = jnp.maximum(peak, jnp.max(scores, axis=1, keepdims=True))
        factor = jnp.exp2(peak - newest)
        sums, weights = None, []
        for at in range(0, scores.shape[1], lanes):
            tile = jnp.exp2(scores[:, at : at + lanes] - newest)
            if valid is not None:
                tile = jnp.where(valid[:, at : at + lanes], tile, 0.0)
            sums = tile if sums is None else sums + tile
            weights.append(tile.astype(jnp.bfloat16))
        total[part, :] = total[part, :] * factor + sums
        acc[part, :] = acc[part, :] * factor + jnp.dot(
            jnp.concatenate(weights, axis=1), block_values, preferred_element_type=jnp.float32
        )
        top[part, :] = newest

    def score(part, block_keys):
        return (
            lax.dot_general(
                q[part, :], block_keys, (((1,), (1,)), ((), ())), preferred_element_type=jnp.float32
            )
            * scale
        )

    def sweep(block_keys, block_values, valid_of):
        parts = [slice(at, at + some) for at in range(0, every, some)]
        ready = score(parts[0], block_keys)
        for number, part in enumerate(parts):
            scores = ready
            if number + 1 < len(parts):
                ready = score(parts[number + 1], block_keys)
            fold(part, scores, valid_of(part), block_values)

    @pl.when(step == 0)
    def _():
        sources = pieces // sequences
        extent = land.shape[2]
        columns = pl.ds(pl.multiple_of(own_head * extent, lanes), extent)
        for piece in range(pieces):

            @pl.when(order[piece] // sources == own_sequence)
            def _(piece=piece):
                land[order[piece] % sources] = blocks[piece][:, columns]

        mine = land[...].reshape(rows, land.shape[2])
        for head in range(group):
            q[head * rows : (head + 1) * rows, :] = mine[:, head * head_size : (head + 1) * head_size]
        own_keys = jnp.concatenate(
            [mine[:, width : width + head_size], jnp.zeros((lanes - rows, head_size), jnp.bfloat16)], 0
        )
        own_values = jnp.concatenate(
            [
                mine[:, width + head_size : width + 2 * head_size],
                jnp.zeros((lanes - rows, head_size), jnp.bfloat16),
            ],
            0,
        )
        seen = jnp.where(is_last > 0, mask[0].astype(jnp.float32), 0.0)
        seen = jnp.concatenate([seen, jnp.zeros((rows, lanes - rows), jnp.float32)], 1)
        valid = jnp.concatenate([seen] * group, 0) > 0.0
        top[...] = jnp.full_like(top, very_low)
        total[...] = jnp.zeros_like(total)
        acc[...] = jnp.zeros_like(acc)
        sweep(own_keys, own_values, lambda part: valid[part, :])

    @pl.when((step + 1) * block <= length)
    def _():
        sweep(keys[...], values[...], lambda part: None)

    @pl.when((step * block < length) & ((step + 1) * block > length))
    def _():
        at = step * block + lax.broadcasted_iota(jnp.int32, (1, block), 1)
        valid = jnp.broadcast_to(at < length, (some, block))
        sweep(keys[...], values[...], lambda part: valid)

    @pl.when(step == pl.num_programs(0) - 1)
    def _():
        summed = jnp.sum(total[...], axis=1, keepdims=True)
        result = acc[...] / summed
        level = top[...] + jnp.log2(summed)
        lane = lax.broadcasted_iota(jnp.int32, (rows, lanes), 1)
        notes = jnp.zeros((rows, lanes), jnp.float32)
        for head in range(group):
            part = slice(head * rows, (head + 1) * rows)
            out[:, head * head_size : (head + 1) * head_size] = result[part].astype(jnp.bfloat16)
            rest = jnp.broadcast_to(level[part, :1], (rows, lanes))
            for piece in range(3):
                cut = rest.astype(jnp.bfloat16).astype(jnp.float32)
                notes = jnp.where(lane == piece * group + head, cut, notes)
                rest = rest - cut
        out[:, width:] = notes.astype(jnp.bfloat16)


def attention(info, order, blocks, mask, keys, values, group):
    head_size = keys.shape[1]
    sequences, rows = mask.shape[0], mask.shape[1]
    capacity = keys.shape[0]
    block = min(1024, capacity)
    width = group * head_size
    pieces = len(blocks)
    extent = width + 2 * head_size

    def at(step, info, order):
        return (jnp.minimum(step, (info[0] + block - 1) // block - 1), 0)

    return pl.pallas_call(
        functools.partial(attention_kernel, pieces, sequences, rows, group, head_size),
        out_shape=jax.ShapeDtypeStruct((rows, width + lanes), jnp.bfloat16),
        grid_spec=pltpu.PrefetchScalarGridSpec(
            num_scalar_prefetch=2,
            grid=(capacity // block,),
            in_specs=[pl.BlockSpec(memory_space=pltpu.VMEM)] * pieces
            + [
                pl.BlockSpec((1, rows, rows), lambda step, info, order: (info[1], 0, 0)),
                pl.BlockSpec((block, head_size), at),
                pl.BlockSpec((block, head_size), at),
            ],
            out_specs=pl.BlockSpec((rows, width + lanes), lambda step, info, order: (0, 0)),
            scratch_shapes=[
                pltpu.VMEM((pieces // sequences, blocks[0].shape[0], extent), jnp.bfloat16),
                pltpu.VMEM((group * rows, head_size), jnp.bfloat16),
                pltpu.VMEM((group * rows, lanes), jnp.float32),
                pltpu.VMEM((group * rows, lanes), jnp.float32),
                pltpu.VMEM((group * rows, head_size), jnp.float32),
            ],
        ),
        compiler_params=pltpu.CompilerParams(vmem_limit_bytes=16 << 20),
        cost_estimate=pl.CostEstimate(
            flops=4 * group * rows * capacity * head_size,
            bytes_accessed=4 * capacity * head_size,
            transcendentals=group * rows * capacity,
        ),
        name="attention",
    )(info, order, *blocks, mask, keys, values)


def projection_kernel(pieces, per_pair, key_heads, sequences, group, head_size, *refs):
    where_from = refs[0]
    blocks = refs[1 : 1 + pieces]
    weight = refs[1 + pieces]
    out = refs[2 + pieces]
    held, attended = refs[3 + pieces :]
    rows = held.shape[1]
    width = group * head_size
    for piece in range(pieces):
        held[piece] = blocks[piece][...]
    result = None
    for head in range(key_heads):
        for sequence in range(sequences):
            pair = sequence * key_heads + head
            slots = [where_from[pair * per_pair + number] for number in range(per_pair)]
            levels = []
            for slot in slots:
                notes = held[slot, :, width:].astype(jnp.float32)
                levels.append(
                    notes
                    + pltpu.roll(notes, lanes - group, 1)
                    + pltpu.roll(notes, lanes - 2 * group, 1)
                )
            highest = functools.reduce(jnp.maximum, levels)
            mixing = [jnp.exp2(level - highest) for level in levels]
            whole = functools.reduce(jnp.add, mixing)
            mixing = [part / whole for part in mixing]
            for member in range(group):
                columns = slice(member * head_size, (member + 1) * head_size)
                gathered = held[slots[-1], :, columns].astype(jnp.float32)
                base = gathered
                for slot, part in zip(slots[:-1], mixing):
                    change = held[slot, :, columns].astype(jnp.float32) - base
                    gathered = gathered + part[:, member : member + 1] * change
                attended[
                    sequence * rows : (sequence + 1) * rows,
                    head * width + member * head_size : head * width + (member + 1) * head_size,
                ] = gathered.astype(jnp.bfloat16)
        part = slice(head * width, (head + 1) * width)
        term = jnp.dot(attended[:, part], weight[part, :], preferred_element_type=jnp.float32)
        result = term if result is None else result + term
    out[...] = result.astype(jnp.bfloat16)


def projection(where_from, blocks, weight, per_pair, key_heads, sequences, group, head_size):
    pieces = len(blocks)
    rows, extent = blocks[0].shape
    return pl.pallas_call(
        functools.partial(
            projection_kernel, pieces, per_pair, key_heads, sequences, group, head_size
        ),
        out_shape=pltpu.VMEM((sequences * rows, weight.shape[1]), jnp.bfloat16),
        in_specs=[pl.BlockSpec(memory_space=pltpu.SMEM)]
        + [pl.BlockSpec(memory_space=pltpu.VMEM)] * (pieces + 1),
        out_specs=pl.BlockSpec(memory_space=pltpu.VMEM),
        scratch_shapes=[
            pltpu.VMEM((pieces, rows, extent), jnp.bfloat16),
            pltpu.VMEM((sequences * rows, weight.shape[0]), jnp.bfloat16),
        ],
        compiler_params=pltpu.CompilerParams(vmem_limit_bytes=16 << 20),
        cost_estimate=pl.CostEstimate(
            flops=2 * sequences * rows * weight.size,
            bytes_accessed=2 * (weight.size + pieces * rows * extent),
            transcendentals=0,
        ),
        name="projection",
    )(where_from, *blocks, weight)


def feed_kernel(slots, total_width, first, last, order, *refs):
    blocks, refs = refs[: len(slots)], refs[len(slots) :]
    (gain, *weights), refs = refs[:3], refs[3:]
    if not first:
        given, refs = refs[:3], refs[3:]
    if last:
        out, totals = refs[0], refs[1:]
    else:
        totals, kept = refs[:2], refs[2]
    if first:
        refs[3][...] = blocks[0][...]
    rows, depth = blocks[0].shape
    squares = jnp.zeros((rows, lanes), jnp.float32) if first else given[2][...]
    for number, (slot, block) in enumerate(zip(slots, blocks)):
        branch = block[...].astype(jnp.float32)
        square = branch * branch
        for at in range(0, depth, lanes):
            squares = squares + square[:, at : at + lanes]
        scaled = (branch * gain[order[slot]]).astype(jnp.bfloat16)
        part = pl.ds(pl.multiple_of(order[slot] * depth, depth), depth)
        for which in range(2):
            term = jnp.dot(scaled, weights[which][part, :], preferred_element_type=jnp.float32)
            if number > 0:
                term = totals[which][...] + term
            elif not first:
                term = given[which][...] + term
            totals[which][...] = term
    if not last:
        kept[...] = squares
        return
    inverse = lax.rsqrt(jnp.sum(squares, axis=1, keepdims=True) / total_width + epsilon)
    opened = totals[0][...] * inverse
    out[...] = (opened / (1.0 + jnp.exp(-opened)) * (totals[1][...] * inverse)).astype(jnp.bfloat16)


def feed(order, blocks, gain, gate_weight, up_weight, mark):
    pieces = len(blocks)
    rows, depth = blocks[0].shape
    width = gate_weight.shape[1]
    far = pieces // 4
    late = [far + number for number in range(1, far, 2)]
    final = [2 * far + number for number in late]
    stages = [[0, 2 * far], [2, 2 * far + 2, far, 3 * far]]
    known = late + final + stages[0] + stages[1]
    stages = stages + [[slot for slot in range(pieces) if slot not in known], late, final]
    whole = pl.BlockSpec(memory_space=pltpu.VMEM)
    table = gain.reshape(pieces, 1, depth)
    result = ()
    for number, slots in enumerate(stages):
        first, last = number == 0, number == len(stages) - 1
        sums = [jax.ShapeDtypeStruct((rows, width), jnp.float32)] * 2
        sums = sums + [jax.ShapeDtypeStruct((rows, lanes), jnp.float32)]
        if first:
            sums = sums + [jax.ShapeDtypeStruct((rows, depth), jnp.bfloat16)]
        shape = jax.ShapeDtypeStruct((rows, width), jnp.bfloat16) if last else tuple(sums)
        kernel = functools.partial(feed_kernel, slots, pieces * depth, first, last)
        result = pl.pallas_call(
            kernel if not last else lambda *refs: kernel(*refs[:-4], *refs[-3:]),
            out_shape=shape,
            in_specs=[pl.BlockSpec(memory_space=pltpu.SMEM)]
            + [whole] * (len(slots) + 3 + len(result) + last),
            out_specs=whole if last else (whole,) * len(shape),
            scratch_shapes=[pltpu.VMEM((rows, width), jnp.float32)] * 2 if last else [],
            compiler_params=pltpu.CompilerParams(vmem_limit_bytes=12 << 20),
            cost_estimate=pl.CostEstimate(
                flops=4 * rows * len(slots) * depth * width,
                bytes_accessed=2 * rows * len(slots) * depth,
                transcendentals=0,
            ),
        )(
            order,
            *[blocks[slot] for slot in slots],
            table,
            gate_weight,
            up_weight,
            *result,
            *((mark,) if last else ()),
        )
        if first:
            result, own = result[:3], result[3]
    return own, result


def mark_kernel(block, out):
    out[...] = block[: out.shape[0], : out.shape[1]]


def marked(block, work):
    whole = pl.BlockSpec(memory_space=pltpu.VMEM)
    return pl.pallas_call(
        mark_kernel,
        out_shape=jax.ShapeDtypeStruct((8, lanes), block.dtype),
        in_specs=[whole],
        out_specs=whole,
        compiler_params=pltpu.CompilerParams(vmem_limit_bytes=1 << 20),
        cost_estimate=pl.CostEstimate(flops=work, bytes_accessed=0, transcendentals=work // 512),
        name="mark",
    )(block)


def spread(block, devices):
    def swap(value, bits):
        return lax.ppermute(value, "wide", [(i, i ^ bits) for i in range(devices)])

    found = [block] + [swap(block, 4 * far) for far in range(1, devices // 4)]
    found = found + [swap(value, 2) for value in found]
    return found + [swap(value, 1) for value in found]


def origins(devices, own_index):
    far = devices // 4
    number = jnp.arange(devices, dtype=jnp.int32)
    swapped = number // far
    return own_index ^ (number % far * 4 + swapped % 2 * 2 + swapped // 2)


def per_device(
    queries,
    draft_keys,
    draft_values,
    cache_keys,
    cache_values,
    block_owner,
    block_lengths,
    draft_mask,
    out_weight,
    norm_gain,
    gate_weight,
    up_weight,
):
    devices = lax.axis_size("wide")
    own_index = lax.axis_index("wide").astype(jnp.int32)
    local_rows = queries.shape[0]
    head_size = cache_keys.shape[1]
    key_heads = draft_keys.shape[1] // head_size
    group_width = queries.shape[1] // key_heads
    group = group_width // head_size
    sequences = draft_mask.shape[0]
    local_rows = queries.shape[0]
    per_pair = devices // (sequences * key_heads)
    device_ids = jnp.arange(devices, dtype=jnp.int32)
    pair = device_ids // per_pair
    facts = jnp.stack(
        [block_lengths, pair // key_heads, pair % key_heads, device_ids % per_pair // (per_pair - 1)]
        if per_pair > 1
        else [block_lengths, pair // key_heads, pair % key_heads, jnp.ones_like(device_ids)]
    )
    info = jnp.sum(jnp.where((block_owner == own_index)[None, :], facts, 0), axis=1)
    order = origins(devices, own_index)
    slot_of = jnp.sum(
        (block_owner[:, None] == order[None, :]).astype(jnp.int32) * device_ids[None, :], axis=1
    )

    packed = jnp.concatenate(
        [
            queries.reshape(local_rows, key_heads, group_width),
            draft_keys.reshape(local_rows, key_heads, head_size),
            draft_values.reshape(local_rows, key_heads, head_size),
        ],
        axis=2,
    ).reshape(local_rows, -1)
    inputs = spread(packed, devices)
    block = attention(
        info,
        order,
        inputs,
        pltpu.with_memory_space_constraint(draft_mask, pltpu.HBM),
        pltpu.with_memory_space_constraint(cache_keys, pltpu.HBM),
        pltpu.with_memory_space_constraint(cache_values, pltpu.HBM),
        group,
    )
    work = 64 * 2 * queries.shape[1] * cache_keys.size // 8
    mark = marked(block, work)
    projected = projection(
        slot_of,
        spread(block, devices),
        pltpu.with_memory_space_constraint(out_weight, pltpu.VMEM),
        per_pair,
        key_heads,
        sequences,
        group,
        head_size,
    )
    projected, hidden = feed(
        order, spread(projected, devices), norm_gain, gate_weight, up_weight, mark
    )
    return (projected, hidden)


def solution(mesh):
    placed = (
        P(("grp", "wide"), None),
        P(("grp", "wide"), None),
        P(("grp", "wide"), None),
        P(("grp", "wide"), None),
        P(("grp", "wide"), None),
        P("grp"),
        P("grp"),
        P("grp", None, None),
        P(None, "wide"),
        P(),
        P(None, "wide"),
        P(None, "wide"),
    )
    return jax.shard_map(
        per_device,
        mesh=mesh,
        in_specs=placed,
        out_specs=(P("grp", "wide"), P("grp", "wide")),
        check_vma=False,
    )
```
